32 devices in a mesh: dp: 8 (over z, y), tensor: 4 (over x, core).
Axes of the slice: x: 2, y: 2, z: 4, core: 2. Of those that a mesh axis runs over, the one named last changes fastest.
Arguments:
- tokens: bfloat16 [5120, 1536], P(('dp', 'tensor')), may hold values from -6 to 6
- cotangent: bfloat16 [5120, 1536], P(('dp', 'tensor')), may hold values from -6 to 6
- master: float32 [4, 8, 2482320], P('tensor', 'dp'), may hold values from -4.2 to 4.2
- first_moment: float32 [4, 8, 2482320], P('tensor', 'dp'), may hold values from -108 to 108
- second_moment: float32 [4, 8, 2482320], P('tensor', 'dp'), may hold values from 100 to 1000
- gain_master: float32 [6272], P(('dp', 'tensor')), may hold values from 0.28 to 2.4
- gain_first: float32 [6272], P(('dp', 'tensor')), may hold values from -108 to 108
- gain_second: float32 [6272], P(('dp', 'tensor')), may hold values from 1000 to 100000
Outputs:
- outputs: bfloat16 [5120, 1536], P(('dp', 'tensor'))
- input_grad: float32 [5120, 1536], P(('dp', 'tensor'))
- weight_grad: float32 [4, 8, 2482320], P('tensor', 'dp')
- new_master: float32 [4, 8, 2482320], P('tensor', 'dp')
- new_first: float32 [4, 8, 2482320], P('tensor', 'dp')
- new_second: float32 [4, 8, 2482320], P('tensor', 'dp')
- new_copy: bfloat16 [4, 8, 2482320], P('tensor', 'dp')
- gain_grad: float32 [6272], P(('dp', 'tensor'))
- new_gain_master: float32 [6272], P(('dp', 'tensor'))
- new_gain_first: float32 [6272], P(('dp', 'tensor'))
- new_gain_second: float32 [6272], P(('dp', 'tensor'))
- norms: float32 [2, 19], replicated
The draws below stay inside these ranges and needn't reach their ends.
All inputs are finite; a program needn't handle non-finite values.
Results may differ from the reference program's by a relative error of at most 0.028.
The reference program's roundings to bfloat16 on the way count: a program that leaves them out, or rounds other values in their place, can miss the bound.
Values may be sent and summed in bfloat16 or wider, within the bound.
No kernel may reach another device: no remote copies, remote signals or barrier semaphores. Data moves between devices by JAX's collectives and lax.ppermute only.
A program may use at most 448 MiB of HBM per device.

```python
import math
import jax
import jax.numpy as jnp
import numpy as np
from jax import lax

MODEL_DIM = 1536
FEED_HIDDEN = 6912
QUERY_HEADS = 24
KEY_VALUE_HEADS = 8
HEAD_DIM = 64
SEQ = 640
TOKENS = 5120
SHARD = 2482320
GAINS = 6272
N_DP = 8
N_TENSOR = 4


def matrix_scales():
    conv_width = MODEL_DIM // N_TENSOR
    hidden_width = FEED_HIDDEN // N_TENSOR
    query_width = QUERY_HEADS // N_TENSOR * HEAD_DIM
    key_value_width = KEY_VALUE_HEADS // N_TENSOR * HEAD_DIM
    attn_boost = max(SEQ, 16) ** 0.5 / 4.0
    feed_entries = [((MODEL_DIM, hidden_width), MODEL_DIM ** (-0.5)), ((MODEL_DIM, hidden_width), MODEL_DIM ** (-0.5)), ((hidden_width, MODEL_DIM), FEED_HIDDEN ** (-0.5))]
    entries = [((MODEL_DIM, 3, conv_width), MODEL_DIM ** (-0.5)), ((3, conv_width), 3 ** (-0.5)), ((conv_width, MODEL_DIM), MODEL_DIM ** (-0.5))]
    entries = entries + feed_entries
    entries = entries + [((MODEL_DIM, query_width), MODEL_DIM ** (-0.5)), ((MODEL_DIM, key_value_width), MODEL_DIM ** (-0.5)), ((MODEL_DIM, key_value_width), MODEL_DIM ** (-0.5)), ((query_width, MODEL_DIM), attn_boost * (QUERY_HEADS * HEAD_DIM) ** (-0.5))]
    entries = entries + feed_entries
    span_list = [math.prod(mat_shape) // N_DP for mat_shape, std_dev in entries]
    return np.repeat(np.array([std_dev for mat_shape, std_dev in entries], np.float32), span_list)


def rising(count):
    return 0.6 * 3.0 ** (jnp.arange(count, dtype=jnp.float32) / max(count - 1, 1))


def base_noise(key, shape):
    noise = jnp.clip(jax.random.normal(key, shape, jnp.float32), -4.0, 4.0)
    return noise


def draw_master(key, part):
    noise = base_noise(jax.random.fold_in(key, 11), (N_TENSOR, N_DP, SHARD))
    return noise * jnp.asarray(matrix_scales())[None, None, :] * rising(N_DP)[None, :, None]


def draw_first_moment(key, part):
    noise = base_noise(jax.random.fold_in(key, 23), (N_TENSOR, N_DP, SHARD))
    return 15.0 * noise * rising(N_DP)[None, :, None]


def draw_gain_master(key, part):
    position = jnp.arange(GAINS, dtype=jnp.float32) / GAINS
    noise = base_noise(jax.random.fold_in(key, 37), (GAINS,))
    return (0.7 + 0.8 * position) * (1.0 + 0.15 * noise)


def draw_gain_first(key, part):
    position = jnp.arange(GAINS, dtype=jnp.float32) / max(GAINS - 1, 1)
    noise = base_noise(jax.random.fold_in(key, 41), (GAINS,))
    return 15.0 * noise * (0.6 * 3.0 ** position)


def draw_gain_second(key, part):
    level = jax.random.uniform(jax.random.fold_in(key, 53), (GAINS,), jnp.float32, 0.0, 1.0)
    return 10.0 ** (3.0 + 2.0 * level)


def steps_of(stream_key, dims, cuts, low, top_value):
    def one(dim, blocks):
        steps = jax.random.uniform(jax.random.fold_in(jax.random.fold_in(stream_key, 6), dim), (blocks,), jnp.float32, low / len(cuts), top_value / len(cuts))
        return jnp.repeat(jnp.exp(steps), dims[dim] // blocks).reshape((-1,) + (1,) * (len(dims) - dim - 1))

    gain = one(*cuts[0])
    for cut in cuts[1:]:
        gain = gain * one(*cut)
    return gain


def scatter_about(own_key, dims, scale, reach, cuts=(), kind=jnp.bfloat16):
    values = scale * jax.random.normal(own_key, dims, jnp.float32)
    if cuts:
        values = values * steps_of(own_key, dims, cuts, -0.22, 0.18)
    return jnp.clip(values, -reach, reach).astype(kind)


def setup_inputs(seed: int = 0) -> dict:
    key_list = jax.random.split(jax.random.key(seed), 9)
    return {
        "tokens": scatter_about(key_list[0], (TOKENS, MODEL_DIM), 1.0, 6.0, ((0, 32),)),
        "cotangent": scatter_about(key_list[1], (TOKENS, MODEL_DIM), 1.0, 6.0, ((0, 32),)),
        "master": draw_master(jax.random.fold_in(key_list[8], 71), 0),
        "first_moment": draw_first_moment(jax.random.fold_in(key_list[8], 71), 0),
        "second_moment": jnp.clip(jnp.exp(math.log(1000.0) - 2.3025851 * jax.random.uniform(key_list[4], (N_TENSOR, N_DP, SHARD), jnp.float32) ** steps_of(key_list[4], (N_TENSOR, N_DP, SHARD), ((0, 4), (1, 8)), -0.2, 0.2)), 100.0, 1000.0),
        "gain_master": draw_gain_master(jax.random.fold_in(key_list[8], 71), 0),
        "gain_first": draw_gain_first(jax.random.fold_in(key_list[8], 71), 0),
        "gain_second": draw_gain_second(jax.random.fold_in(key_list[8], 71), 0),
    }


@jax.custom_vjp
def lower_precision(v):
    return lax.optimization_barrier(v.astype(jnp.bfloat16)).astype(jnp.float32)

@jax.custom_vjp
def lower_backward(v):
    return v

def low_keep(v):
    return (lower_precision(v), None)

def low_pass(kept, grad):
    return (grad,)

def back_keep(v):
    return (v, None)

def back_low(kept, grad):
    return (lower_precision(grad),)
lower_precision.defvjp(low_keep, low_pass)
lower_backward.defvjp(back_keep, back_low)
NORM_EPS = 1e-05
ROPE_BASE = 1000000.0
TOP_PRECISION = lax.Precision.HIGHEST
BETA_FIRST = 0.9
BETA_SECOND = 0.99
ADAM_EPS = 1e-06
DECAY = 0.01
LEARN_RATE = 0.25
TRUST_EPS = 1e-06
MASK_FILL = -1e+30

def weight_layout(model_width, conv_width, hidden_width, query_width, key_value_width):
    feed_shapes = [((model_width, hidden_width), 1), ((model_width, hidden_width), 1), ((hidden_width, model_width), 0)]
    return [[((model_width, 3, conv_width), 2), ((3, conv_width), 1), ((conv_width, model_width), 0)], feed_shapes, [((model_width, query_width), 1), ((model_width, key_value_width), 1), ((model_width, key_value_width), 1), ((query_width, model_width), 0)], feed_shapes]

def matrix_list():
    weight_segments = weight_layout(MODEL_DIM, MODEL_DIM // N_TENSOR, FEED_HIDDEN // N_TENSOR, QUERY_HEADS // N_TENSOR * HEAD_DIM, KEY_VALUE_HEADS // N_TENSOR * HEAD_DIM)
    return [mat_entry for segment in weight_segments for mat_entry in segment]

def unpack(packed):
    result = []
    offset = 0
    for mat_shape, joined in matrix_list():
        span_dev = math.prod(mat_shape) // N_DP
        pieces = [packed[tensor_rank, :, offset:offset + span_dev].reshape(mat_shape) for tensor_rank in range(N_TENSOR)]
        result.append(jnp.concatenate(pieces, axis=joined))
        offset += span_dev
    return result

def pack(matrices):
    per_rank = [[] for tensor_rank in range(N_TENSOR)]
    for (mat_shape, joined), matrix in zip(matrix_list(), matrices):
        pieces = jnp.split(matrix, N_TENSOR, axis=joined)
        for tensor_rank in range(N_TENSOR):
            per_rank[tensor_rank].append(pieces[tensor_rank].reshape(N_DP, -1))
    return jnp.stack([jnp.concatenate(rank_items, axis=1) for rank_items in per_rank])

def rms_norm(values, gain_vec):
    return values * lax.rsqrt(lax.optimization_barrier(jnp.mean(values * values, axis=-1, keepdims=True)) + NORM_EPS) * gain_vec

def rope_tables(sequence_length):
    positions = jnp.arange(sequence_length, dtype=jnp.float32)
    inv_freq = ROPE_BASE ** (-jnp.arange(0, HEAD_DIM, 2, dtype=jnp.float32) / HEAD_DIM)
    angles = positions[:, None] * inv_freq[None, :]
    return (jnp.cos(angles)[:, None, :], jnp.sin(angles)[:, None, :])

def rotate(values, cosines, sines):
    half_dim = values.shape[-1] // 2
    first_half = values[..., :half_dim]
    second_half = values[..., half_dim:]
    return jnp.concatenate([first_half * cosines - second_half * sines, second_half * cosines + first_half * sines], axis=-1)

def conv_mixer(normed, w_in, kernel, w_out):
    lower_rows = lower_precision(normed)
    projected = lower_backward(jnp.einsum('sd,dkc->skc', lower_rows, w_in, precision=TOP_PRECISION))
    gate_b = projected[:, 0]
    gate_c = projected[:, 1]
    values = projected[:, 2]
    product = gate_b * values
    padded = jnp.pad(product, ((2, 0), (0, 0)))
    conv_mixed = kernel[0] * padded[:-2] + kernel[1] * padded[1:-1] + kernel[2] * padded[2:]
    return lower_backward(jnp.dot(lower_precision(gate_c * conv_mixed), w_out, precision=TOP_PRECISION))

def feed_forward(normed, w_gate, w_up, w_down):
    lower_rows = lower_precision(normed)
    gate_vals = lower_backward(jnp.dot(lower_rows, w_gate, precision=TOP_PRECISION))
    up_vals = lower_backward(jnp.dot(lower_rows, w_up, precision=TOP_PRECISION))
    hidden = lower_precision(jax.nn.silu(gate_vals) * up_vals)
    return lower_backward(jnp.dot(hidden, w_down, precision=TOP_PRECISION))

def attention(normed, w_query, key_matrix, value_matrix, w_attn, gain_query, gain_key, cosines, sines):
    sequence_length = normed.shape[0]
    lower_rows = lower_precision(normed)
    query_rows = lower_backward(jnp.dot(lower_rows, w_query, precision=TOP_PRECISION)).reshape(sequence_length, QUERY_HEADS, HEAD_DIM)
    key_head_rows = lower_backward(jnp.dot(lower_rows, key_matrix, precision=TOP_PRECISION)).reshape(sequence_length, KEY_VALUE_HEADS, HEAD_DIM)
    value_head_rows = lower_precision(lower_backward(jnp.dot(lower_rows, value_matrix, precision=TOP_PRECISION))).reshape(sequence_length, KEY_VALUE_HEADS, HEAD_DIM)
    query_rows = lower_precision(rotate(rms_norm(query_rows, gain_query), cosines, sines))
    key_head_rows = lower_precision(rotate(rms_norm(key_head_rows, gain_key), cosines, sines))
    query_group_size = QUERY_HEADS // KEY_VALUE_HEADS
    query_rows = query_rows.reshape(sequence_length, KEY_VALUE_HEADS, query_group_size, HEAD_DIM).transpose(1, 0, 2, 3)
    causal = jnp.arange(sequence_length)[:, None] >= jnp.arange(sequence_length)[None, :]
    score_scale = HEAD_DIM ** (-0.5)

    def one_group(operands):
        query_grp, key_grp, value_grp = operands
        scores = lower_backward(jnp.einsum('sgd,td->gst', query_grp, key_grp, precision=TOP_PRECISION) * score_scale)
        scores = jnp.where(causal[None], scores, MASK_FILL)
        soft_probs = jax.nn.softmax(scores, axis=-1)
        return lower_precision(lower_backward(jnp.einsum('gst,td->sgd', lower_precision(soft_probs), value_grp, precision=TOP_PRECISION)))
    attended = lax.map(jax.checkpoint(one_group), (query_rows, key_head_rows.transpose(1, 0, 2), value_head_rows.transpose(1, 0, 2)))
    attended = attended.transpose(1, 0, 2, 3).reshape(sequence_length, QUERY_HEADS * HEAD_DIM)
    return lower_backward(jnp.dot(attended, w_attn, precision=TOP_PRECISION))

def block(inputs, matrices, gain_vals, cosines, sines):
    w_in, kernel, w_out, gate_one, up_one, down_one, w_query, key_matrix, value_matrix, w_attn, gate_two, up_two, down_two = matrices
    gain_one = gain_vals[0:MODEL_DIM]
    gain_two = gain_vals[MODEL_DIM:2 * MODEL_DIM]
    gain_three = gain_vals[2 * MODEL_DIM:3 * MODEL_DIM]
    gain_four = gain_vals[3 * MODEL_DIM:4 * MODEL_DIM]
    gain_query = gain_vals[4 * MODEL_DIM:4 * MODEL_DIM + HEAD_DIM]
    gain_key = gain_vals[4 * MODEL_DIM + HEAD_DIM:4 * MODEL_DIM + 2 * HEAD_DIM]
    resid_one = inputs + conv_mixer(rms_norm(inputs, gain_one), w_in, kernel, w_out)
    resid_two = resid_one + feed_forward(rms_norm(resid_one, gain_two), gate_one, up_one, down_one)
    resid_three = resid_two + attention(rms_norm(resid_two, gain_three), w_query, key_matrix, value_matrix, w_attn, gain_query, gain_key, cosines, sines)
    return resid_three + feed_forward(rms_norm(resid_three, gain_four), gate_two, up_two, down_two)

def adam_terms(weight, grad_vals, first_old, second_old):
    first_new = BETA_FIRST * first_old + (1.0 - BETA_FIRST) * grad_vals
    second_new = BETA_SECOND * second_old + (1.0 - BETA_SECOND) * grad_vals * grad_vals
    update = first_new / (jnp.sqrt(second_new) + ADAM_EPS) + DECAY * weight
    return (first_new, second_new, update)

def reference(tokens, cotangent, master, first_moment, second_moment, gain_master, gain_first, gain_second):
    matrices = unpack(lower_precision(master))
    cosines, sines = rope_tables(SEQ)
    sequences = tokens.astype(jnp.float32).reshape(N_DP, SEQ, MODEL_DIM)
    seq_cot = cotangent.astype(jnp.float32).reshape(N_DP, SEQ, MODEL_DIM)

    def one_sequence(totals, operands):
        seq_tokens, seq_grad = operands
        primal_out, pullback = jax.vjp(lambda inputs, mat_list, gain_vals: block(inputs, mat_list, gain_vals, cosines, sines), seq_tokens, matrices, gain_master)
        grad_tokens, grad_mats, grad_gains = pullback(seq_grad)
        totals = (jax.tree.map(jnp.add, totals[0], grad_mats), totals[1] + grad_gains)
        return (totals, (primal_out, grad_tokens))
    initial = (jax.tree.map(jnp.zeros_like, matrices), jnp.zeros_like(gain_master))
    (grad_mats, grad_gains), (outputs, grad_tokens) = lax.scan(one_sequence, initial, (sequences, seq_cot))
    weight_grad = pack(grad_mats)
    first_new, second_new, update = adam_terms(master, weight_grad, first_moment, second_moment)
    gain_first_new, gain_second_new, gain_update = adam_terms(gain_master, grad_gains, gain_first, gain_second)
    spans = [math.prod(mat_shape) // N_DP for mat_shape, joined in matrix_list()]
    bounds = np.cumsum([0] + spans)
    weight_sq = jnp.stack([jnp.sum(master[:, :, bounds[number]:bounds[number + 1]] ** 2) for number in range(len(spans))])
    update_sq = jnp.stack([jnp.sum(update[:, :, bounds[number]:bounds[number + 1]] ** 2) for number in range(len(spans))])
    gain_spans = [MODEL_DIM, MODEL_DIM, MODEL_DIM, MODEL_DIM, HEAD_DIM, HEAD_DIM]
    gain_edges = np.cumsum([0] + gain_spans)
    gain_wsq = jnp.stack([jnp.sum(gain_master[gain_edges[number]:gain_edges[number + 1]] ** 2) for number in range(6)])
    gain_usq = jnp.stack([jnp.sum(gain_update[gain_edges[number]:gain_edges[number + 1]] ** 2) for number in range(6)])
    weight_norm = jnp.sqrt(jnp.concatenate([weight_sq, gain_wsq]))
    update_norm = jnp.sqrt(jnp.concatenate([update_sq, gain_usq]))
    trust_ratio = weight_norm / (update_norm + TRUST_EPS)
    mat_count = len(spans)
    mat_ratio = jnp.repeat(trust_ratio[:mat_count], np.array(spans), total_repeat_length=SHARD)
    gain_ratio = jnp.repeat(trust_ratio[mat_count:], np.array(gain_spans), total_repeat_length=GAINS)
    new_master = master - LEARN_RATE * mat_ratio[None, None, :] * update
    new_gain_master = gain_master - LEARN_RATE * gain_ratio * gain_update
    norms = jnp.stack([weight_norm, update_norm])
    return (outputs.reshape(TOKENS, MODEL_DIM).astype(jnp.bfloat16), grad_tokens.reshape(TOKENS, MODEL_DIM), weight_grad, new_master, first_new, second_new, new_master.astype(jnp.bfloat16), grad_gains, new_gain_master, gain_first_new, gain_second_new, norms)
```

```python
import math

import jax
import jax.numpy as jnp
import numpy as np
from jax import lax
from jax.experimental import pallas as pl
from jax.experimental.pallas import tpu as pltpu
from jax.sharding import PartitionSpec as P

MODEL_DIM = 1536
FEED_HIDDEN = 6912
QUERY_HEADS = 24
KEY_VALUE_HEADS = 8
HEAD_DIM = 64


NORM_EPS = 1e-05
ROPE_BASE = 1000000.0
BETA_FIRST = 0.9
BETA_SECOND = 0.99
ADAM_EPS = 1e-06
DECAY = 0.01
LEARN_RATE = 0.25
TRUST_EPS = 1e-06
MASK_FILL = -1e30


def weight_layout(model_width, conv_width, hidden_width, query_width, key_value_width):
    feed_shapes = [
        (model_width, hidden_width),
        (model_width, hidden_width),
        (hidden_width, model_width),
    ]
    return [
        [(model_width, 3, conv_width), (3, conv_width), (conv_width, model_width)],
        feed_shapes,
        [
            (model_width, query_width),
            (model_width, key_value_width),
            (model_width, key_value_width),
            (query_width, model_width),
        ],
        feed_shapes,
    ]


def rms_norm(values, gain_vec):
    return (
        values * lax.rsqrt(jnp.mean(values * values, axis=-1, keepdims=True) + NORM_EPS) * gain_vec
    )


def rotate(values, cosines, sines):
    half_dim = values.shape[-1] // 2
    first_half = values[..., :half_dim]
    second_half = values[..., half_dim:]
    return jnp.concatenate(
        [first_half * cosines - second_half * sines, second_half * cosines + first_half * sines],
        axis=-1,
    )


def head_prep(raw_rows, gain_vec, cosines, sines):
    sequence_length = raw_rows.shape[0]
    return rotate(
        rms_norm(raw_rows.reshape(sequence_length, -1, HEAD_DIM), gain_vec), cosines, sines
    )


def gated_unit(gate_vals, up_vals):
    return jax.nn.silu(gate_vals) * up_vals


def adam_terms(weight, grad_vals, first_old, second_old):
    first_new = BETA_FIRST * first_old + (1.0 - BETA_FIRST) * grad_vals
    second_new = BETA_SECOND * second_old + (1.0 - BETA_SECOND) * grad_vals * grad_vals
    update = first_new / (jnp.sqrt(second_new) + ADAM_EPS) + DECAY * weight
    return (first_new, second_new, update)


def dot_rows(lhs_rows, rhs_matrix):
    return jnp.dot(lhs_rows, rhs_matrix, preferred_element_type=jnp.float32)


def dot_first(lhs_rows, rhs_rows):
    return lax.dot_general(
        lhs_rows, rhs_rows, (((0,), (0,)), ((), ())), preferred_element_type=jnp.float32
    )


def dot_last(lhs_rows, rhs_matrix):
    return lax.dot_general(
        lhs_rows, rhs_matrix, (((1,), (1,)), ((), ())), preferred_element_type=jnp.float32
    )


def norm_back(values, gain_vec, grad_out):
    primal_out, pullback = jax.vjp(rms_norm, values, gain_vec)
    return pullback(grad_out)


TENSOR_ORDER = (0, 2, 1, 3)


def swap(values, axis_name, bit):
    count = lax.axis_size(axis_name)
    return lax.ppermute(values, axis_name, [(i, i ^ bit) for i in range(count)])


def gather_rows(values):
    if lax.axis_size("tensor") != 4:
        return lax.all_gather(values, "tensor", axis=0, tiled=True)
    far = swap(values, "tensor", 2)
    near = swap(values, "tensor", 1)
    return jnp.concatenate([values, far, near, swap(far, "tensor", 1)], axis=0)


def scatter_rows(partial):
    if lax.axis_size("tensor") != 4:
        return lax.psum_scatter(
            partial.astype(jnp.float32), "tensor", scatter_dimension=0, tiled=True
        )
    own, far, near, cross = jnp.split(partial, 4, axis=0)
    far_sum = far.astype(jnp.float32) + swap(cross, "tensor", 1).astype(jnp.float32)
    far_in = swap(far_sum.astype(partial.dtype), "tensor", 2)
    own_sum = own.astype(jnp.float32) + swap(near, "tensor", 1).astype(jnp.float32)
    return own_sum + far_in.astype(jnp.float32)


def block_owners():
    count = lax.axis_size("tensor")
    own = lax.axis_index("tensor")
    return jnp.stack([own ^ bit for bit in TENSOR_ORDER]) if count == 4 else jnp.arange(count)


def gather_sum(lhs_rows, rhs_matrix, send_type=jnp.float32):
    return scatter_rows(dot_rows(lhs_rows, rhs_matrix).astype(send_type))


def sum_input_grads(grad_pairs):
    running = None
    for grad_block, weight in grad_pairs:
        product_part = dot_last(grad_block, weight)
        running = product_part if running is None else running + product_part
    return scatter_rows(running.astype(jnp.bfloat16))


def flip_slots(slots, own):
    count = slots.shape[0]
    rest = slots.shape[1:]
    bit = 1
    while bit < count:
        view = slots.reshape((count // (2 * bit), 2, bit) + rest)
        slots = jnp.where((own & bit) != 0, view[:, ::-1], view).reshape((count,) + rest)
        bit *= 2
    return slots


def gather_small(values, axis_name):
    count = lax.axis_size(axis_name)
    slots = [values] + [swap(values, axis_name, bit) for bit in range(1, count)]
    return flip_slots(jnp.stack(slots), lax.axis_index(axis_name))


def scatter_small(values, axis_name):
    count = lax.axis_size(axis_name)
    slots = flip_slots(values, lax.axis_index(axis_name))
    total = slots[0]
    for bit in range(1, count):
        total = total + swap(slots[bit], axis_name, bit)
    return total


def sum_small(values):
    for axis_name in ("tensor", "dp"):
        values = jnp.sum(gather_small(values, axis_name), axis=0)
    return values


def shift_pairs(step):
    return [(z * 2 + y, (z + step) % 4 * 2 + y) for z in range(4) for y in range(2)]


def fetch_matrix(piece):
    if lax.axis_size("dp") != 8:
        whole = lax.all_gather(piece, "dp", axis=0, tiled=True)
        return whole, ()
    own = lax.axis_index("dp")
    z_own, y_own = own // 2, own % 2
    column = [piece] + [lax.ppermute(piece, "dp", shift_pairs(step)) for step in (1, 2, 3)]
    whole = jnp.zeros((8,) + piece.shape, piece.dtype)
    for step in range(4):
        slot = (z_own + 4 - step) % 4 * 2
        whole = lax.dynamic_update_index_in_dim(whole, column[step], slot + y_own, 0)
        other = swap(column[step], "dp", 1)
        whole = lax.dynamic_update_index_in_dim(whole, other, slot + 1 - y_own, 0)
    return whole.reshape((-1,) + piece.shape[1:]), tuple(column[1:])


def reduce_matrix(grad):
    dp_count = lax.axis_size("dp")
    if dp_count != 8:
        return lax.psum_scatter(grad.astype(jnp.float32), "dp", scatter_dimension=0, tiled=True)
    own = lax.axis_index("dp")
    z_own, y_own = own // 2, own % 2
    blocks = grad.astype(jnp.bfloat16).reshape((4, 2, grad.shape[0] // 8, grad.shape[1]))

    def block(slot, side):
        return lax.dynamic_slice(
            blocks, (slot, side, 0, 0), (1, 1) + blocks.shape[2:]
        ).reshape(blocks.shape[2:])

    total = None
    for step in (1, 2, 3, 0):
        slot = (z_own + step) % 4
        other = swap(block(slot, 1 - y_own), "dp", 1)
        pair = block(slot, y_own).astype(jnp.float32) + other.astype(jnp.float32)
        if step:
            pair = lax.ppermute(pair.astype(jnp.bfloat16), "dp", shift_pairs(step))
            pair = pair.astype(jnp.float32)
        total = pair if total is None else total + pair
    return total


def fetch_all(pieces):
    result = []
    landed = []
    for number, piece in enumerate(pieces):
        if number >= 2 and landed[number - 2]:
            piece, _ = lax.optimization_barrier((piece, landed[number - 2]))
        whole, hops = fetch_matrix(piece)
        landed.append(hops)
        result.append(whole)
    return result


class FlatPlan:
    def __init__(self, spans):
        self.total = sum(spans)
        self.gap = spans[1]
        self.gap_rows, self.gap_lanes = divmod(self.gap, 128)
        self.front = spans[0] // 128
        self.rows = self.front // 3
        self.rest = sum(spans[2:]) // 128
        self.front_blocks = 3
        self.blocks = 3 + -(-(self.rest + self.gap_rows + 1) // self.rows)
        sizes = [spans[0] // 128] + [span // 128 for span in spans[2:]]
        unit = math.gcd(*sizes)
        unit = math.gcd(unit, self.rows)
        while unit % 16 == 0 and unit > 128:
            unit //= 2
        self.unit = unit
        count = len(spans)
        per_block = self.rows // unit
        main = np.full(self.blocks * per_block, count, np.int32)
        edge = np.full(self.blocks * per_block, count, np.int32)
        front_units = self.front // unit
        main[:front_units] = 0
        at = front_units
        edge[at] = 1
        for number in range(2, count):
            units = spans[number] // 128 // unit
            main[at : at + units] = number
            edge[at + 1 : at + units + 1] = number
            at += units
        self.table = np.stack([main, edge])
        self.per_block = per_block
        self.count = count


def flat_spec(plan):
    return pl.BlockSpec((1, 1, plan.rows * 128), lambda i, *_: (0, 0, i))


def rows_spec(plan):
    return pl.BlockSpec((plan.rows, 128), lambda i, *_: (i, 0))


def lane_ids(rows):
    return lax.broadcasted_iota(jnp.int32, (rows, 128), 1)


def to_rows(plan, flat):
    rows, lanes, skip = plan.rows, plan.gap_lanes, plan.gap_rows
    last = -(-plan.total // 1024) - 1

    def body(cur_ref, next_ref, out_ref, work_ref):
        cur = cur_ref[0, 0].reshape(rows, 128)
        work_ref[0:rows, :] = cur
        work_ref[rows : rows + 8, :] = next_ref[0, 0].reshape(8, 128)
        low = pltpu.roll(work_ref[skip : skip + rows, :], 128 - lanes, 1)
        high = pltpu.roll(work_ref[skip + 1 : skip + 1 + rows, :], 128 - lanes, 1)
        moved = jnp.where(lane_ids(rows) < 128 - lanes, low, high)
        front = pl.program_id(0) < plan.front_blocks
        out_ref[...] = jnp.where(front, cur, moved).astype(jnp.bfloat16)

    return pl.pallas_call(
        body,
        name="to_rows",
        grid=(plan.blocks,),
        out_shape=jax.ShapeDtypeStruct((plan.blocks * rows, 128), jnp.bfloat16),
        in_specs=[
            flat_spec(plan),
            pl.BlockSpec(
                (1, 1, 1024), lambda i: (0, 0, jnp.minimum((i + 1) * (rows // 8), last))
            ),
        ],
        out_specs=rows_spec(plan),
        scratch_shapes=[pltpu.VMEM((rows + 8, 128), jnp.float32)],
        cost_estimate=pl.CostEstimate(
            flops=plan.total, bytes_accessed=6 * plan.total, transcendentals=0
        ),
    )(flat, flat)


def edge_mask(plan):
    place = lax.broadcasted_iota(jnp.int32, (8, 128), 0) * 128 + lane_ids(8)
    return (place < plan.gap) & (pl.program_id(0) >= plan.front_blocks)


def moments_pass(plan, weight, first_old, second_old, grad_rows, gap_rows):
    rows, lanes, skip, unit = plan.rows, plan.gap_lanes, plan.gap_rows, plan.unit

    def body(
        table, w_ref, m_ref, v_ref, g_ref, prev_ref, gap_ref,
        grad_ref, first_ref, second_ref, sums_ref, work_ref,
    ):
        step = pl.program_id(0)

        @pl.when(step == 0)
        def _():
            sums_ref[...] = jnp.zeros_like(sums_ref)

        cur = g_ref[...]
        prev = jnp.where(step == plan.front_blocks, gap_ref[...], prev_ref[...])
        work_ref[0:8, :] = pltpu.roll(prev, lanes, 1)
        work_ref[8 : 8 + rows, :] = pltpu.roll(cur, lanes, 1)
        low = work_ref[7 - skip : 7 - skip + rows, :]
        high = work_ref[8 - skip : 8 - skip + rows, :]
        moved = jnp.where(lane_ids(rows) < lanes, low, high)
        grad = jnp.where(step < plan.front_blocks, cur, moved)
        w = w_ref[0, 0].reshape(rows, 128)
        first_new, second_new, update = adam_terms(
            w, grad, m_ref[0, 0].reshape(rows, 128), v_ref[0, 0].reshape(rows, 128)
        )
        grad_ref[0, 0] = grad.reshape(rows * 128)
        first_ref[0, 0] = first_new.reshape(rows * 128)
        second_ref[0, 0] = second_new.reshape(rows * 128)
        mask = edge_mask(plan)
        for part in range(plan.per_block):
            main = table[0, step * plan.per_block + part]
            edge = table[1, step * plan.per_block + part]
            for base, values in ((0, w), (plan.count + 1, update)):
                square = values[part * unit : (part + 1) * unit]
                square = square * square
                inner = jnp.where(mask, 0.0, square[0:8])
                for at in range(8, unit, 8):
                    inner = inner + square[at : at + 8]
                sums_ref[base + main] += inner
                sums_ref[base + edge] += jnp.where(mask, square[0:8], 0.0)

    lin = flat_spec(plan)
    flat = jax.ShapeDtypeStruct((1, 1, plan.total), jnp.float32)
    sums = 2 * (plan.count + 1)
    return pl.pallas_call(
        body,
        name="moments_pass",
        grid_spec=pltpu.PrefetchScalarGridSpec(
            num_scalar_prefetch=1,
            grid=(plan.blocks,),
            in_specs=[
                lin, lin, lin, rows_spec(plan),
                pl.BlockSpec(
                    (8, 128), lambda i, *_: (jnp.maximum(i * (rows // 8) - 1, 0), 0)
                ),
                pl.BlockSpec((8, 128), lambda i, *_: (0, 0)),
            ],
            out_specs=[lin, lin, lin, pl.BlockSpec((sums, 8, 128), lambda i, *_: (0, 0, 0))],
            scratch_shapes=[pltpu.VMEM((rows + 8, 128), jnp.float32)],
        ),
        out_shape=[flat, flat, flat, jax.ShapeDtypeStruct((sums, 8, 128), jnp.float32)],
        cost_estimate=pl.CostEstimate(
            flops=20 * plan.total, bytes_accessed=28 * plan.total, transcendentals=plan.total
        ),
    )(jnp.asarray(plan.table), weight, first_old, second_old, grad_rows, grad_rows, gap_rows)


def weights_pass(plan, weight, first_new, second_new, ratios):
    rows, unit = plan.rows, plan.unit

    def body(table, w_ref, m_ref, v_ref, ratio_ref, new_ref, copy_ref):
        step = pl.program_id(0)
        mask = edge_mask(plan)
        pieces = []
        w = w_ref[0, 0].reshape(rows, 128)
        first, second = m_ref[0, 0].reshape(rows, 128), v_ref[0, 0].reshape(rows, 128)
        update = first / (jnp.sqrt(second) + ADAM_EPS) + DECAY * w
        for part in range(plan.per_block):
            main = ratio_ref[table[0, step * plan.per_block + part]]
            edge = ratio_ref[table[1, step * plan.per_block + part]]
            here = slice(part * unit, part * unit + 8)
            pieces.append(w[here] - LEARN_RATE * jnp.where(mask, edge, main) * update[here])
            here = slice(part * unit + 8, (part + 1) * unit)
            pieces.append(w[here] - LEARN_RATE * main * update[here])
        fresh = jnp.concatenate(pieces, axis=0)
        new_ref[0, 0] = fresh.reshape(rows * 128)
        copy_ref[0, 0] = fresh.reshape(rows * 128).astype(jnp.bfloat16)

    lin = flat_spec(plan)
    shape = (1, 1, plan.total)
    return pl.pallas_call(
        body,
        name="weights_pass",
        grid_spec=pltpu.PrefetchScalarGridSpec(
            num_scalar_prefetch=1,
            grid=(plan.blocks,),
            in_specs=[lin, lin, lin, pl.BlockSpec(memory_space=pltpu.SMEM)],
            out_specs=[lin, lin],
        ),
        out_shape=[
            jax.ShapeDtypeStruct(shape, jnp.float32),
            jax.ShapeDtypeStruct(shape, jnp.bfloat16),
        ],
        cost_estimate=pl.CostEstimate(
            flops=8 * plan.total, bytes_accessed=18 * plan.total, transcendentals=plan.total
        ),
    )(jnp.asarray(plan.table), weight, first_new, second_new, ratios)


def neighbour_rows(edge_rows, owners, offset):
    result = []
    for here in range(edge_rows.shape[0]):
        picked = jnp.zeros_like(edge_rows[0])
        for there in range(edge_rows.shape[0]):
            hit = owners[there] == owners[here] + offset
            picked = jnp.where(hit, edge_rows[there], picked)
        result.append(picked)
    return jnp.stack(result)


def mixer_forward(residual, gain_vec, weights, owners):
    w_in, kernel, w_out = weights
    conv_width = kernel.shape[1]
    normed_rows = gather_rows(rms_norm(residual, gain_vec).astype(jnp.bfloat16))
    projected = dot_rows(normed_rows, w_in).reshape(owners.shape[0], -1, 3 * conv_width)
    gate_b = projected[:, :, :conv_width]
    gate_c = projected[:, :, conv_width : 2 * conv_width]
    values = projected[:, :, 2 * conv_width :]
    product = gate_b * values
    padded = jnp.concatenate([neighbour_rows(product[:, -2:], owners, -1), product], axis=1)
    conv_mixed = (
        kernel[0] * padded[:, :-2] + kernel[1] * padded[:, 1:-1] + kernel[2] * padded[:, 2:]
    )
    conv_out = (gate_c * conv_mixed).astype(jnp.bfloat16).reshape(-1, conv_width)
    kept_vals = (normed_rows, gate_b, gate_c, values, padded, conv_mixed, conv_out)
    return (residual + gather_sum(conv_out, w_out), kept_vals)


def mixer_backward(grad_out, residual, gain_vec, weights, kept_vals, owners):
    w_in, kernel, w_out = weights
    normed_rows, gate_b, gate_c, values, padded, conv_mixed, conv_out = kept_vals
    grad_rows = gather_rows(grad_out.astype(jnp.bfloat16))
    d_conv = dot_last(grad_rows, w_out).reshape(conv_mixed.shape)
    d_gate_c = d_conv * conv_mixed
    d_mixed = d_conv * gate_c
    padded_grad = jnp.concatenate([d_mixed, neighbour_rows(d_mixed[:, :2], owners, 1)], axis=1)
    d_product = (
        kernel[0] * padded_grad[:, 2:]
        + kernel[1] * padded_grad[:, 1:-1]
        + kernel[2] * padded_grad[:, :-2]
    )
    d_kernel = jnp.stack(
        [
            jnp.sum(d_mixed * padded[:, :-2], axis=(0, 1)),
            jnp.sum(d_mixed * padded[:, 1:-1], axis=(0, 1)),
            jnp.sum(d_mixed * padded[:, 2:], axis=(0, 1)),
        ]
    )
    d_proj = jnp.concatenate(
        [
            (d_product * values).astype(jnp.bfloat16),
            d_gate_c.astype(jnp.bfloat16),
            (d_product * gate_b).astype(jnp.bfloat16),
        ],
        axis=-1,
    ).reshape(normed_rows.shape[0], -1)
    d_normed = sum_input_grads(((d_proj, w_in),))
    d_resid, d_gain = norm_back(residual, gain_vec, d_normed)
    grads = (grad_product(normed_rows, d_proj), grad_product(conv_out, grad_rows))
    return (grad_out + d_resid, d_gain, d_kernel, grads)


def grad_product(lhs_rows, rhs_rows):
    return reduce_matrix(dot_first(lhs_rows, rhs_rows).astype(jnp.bfloat16))


def ffn_forward(residual, gain_vec, weights, send_type=jnp.float32):
    w_gate, w_up, w_down = weights
    normed_rows = gather_rows(rms_norm(residual, gain_vec).astype(jnp.bfloat16))
    gate_vals = dot_rows(normed_rows, w_gate)
    up_vals = dot_rows(normed_rows, w_up)
    hidden = gated_unit(gate_vals, up_vals).astype(jnp.bfloat16)
    return (residual + gather_sum(hidden, w_down, send_type), (normed_rows, gate_vals, up_vals, hidden))


def ffn_backward(grad_out, residual, gain_vec, weights, kept_vals):
    w_gate, w_up, w_down = weights
    normed_rows, gate_vals, up_vals, hidden = kept_vals
    grad_rows = gather_rows(grad_out.astype(jnp.bfloat16))
    grad_down = grad_product(hidden, grad_rows)
    d_hidden = dot_last(grad_rows, w_down)
    primal_out, pullback = jax.vjp(gated_unit, gate_vals, up_vals)
    d_gate, d_up = pullback(d_hidden)
    d_gate = d_gate.astype(jnp.bfloat16)
    d_up = d_up.astype(jnp.bfloat16)
    d_normed = sum_input_grads(((d_gate, w_gate), (d_up, w_up)))
    d_resid, d_gain = norm_back(residual, gain_vec, d_normed)
    grads = (grad_product(normed_rows, d_gate), grad_product(normed_rows, d_up), grad_down)
    return (grad_out + d_resid, d_gain, grads)


def rope_tables_at(positions):
    inv_freq = ROPE_BASE ** (-jnp.arange(0, HEAD_DIM, 2, dtype=jnp.float32) / HEAD_DIM)
    angles = positions.astype(jnp.float32)[:, None] * inv_freq[None, :]
    return (jnp.cos(angles)[:, None, :], jnp.sin(angles)[:, None, :])


def score_block(query_b, key_b, causal):
    scores = jnp.einsum(
        "snge,tne->ngst", query_b, key_b, preferred_element_type=jnp.float32
    ) * HEAD_DIM ** (-0.5)
    return jnp.where(causal, scores, MASK_FILL)


def attention_forward(residual, gain_vec, gain_query, gain_key, weights, tables, causal):
    w_qkv, w_attn = weights
    cosines, sines = tables
    normed_rows = gather_rows(rms_norm(residual, gain_vec).astype(jnp.bfloat16))
    seq_len = normed_rows.shape[0]
    q_width = w_attn.shape[0]
    k_width = (w_qkv.shape[1] - q_width) // 2
    q_heads = q_width // HEAD_DIM
    kv_heads = k_width // HEAD_DIM
    projected = dot_rows(normed_rows, w_qkv)
    query_raw = projected[:, :q_width]
    key_raw = projected[:, q_width : q_width + k_width]
    value_b = (
        projected[:, q_width + k_width :]
        .astype(jnp.bfloat16)
        .reshape(seq_len, kv_heads, HEAD_DIM)
    )
    query_b = (
        head_prep(query_raw, gain_query, cosines, sines)
        .astype(jnp.bfloat16)
        .reshape(seq_len, kv_heads, q_heads // kv_heads, HEAD_DIM)
    )
    key_b = head_prep(key_raw, gain_key, cosines, sines).astype(jnp.bfloat16)
    scores = score_block(query_b, key_b, causal)
    top_score = jnp.max(scores, axis=-1, keepdims=True)
    exp_scores = jnp.exp(scores - top_score)
    exp_total = jnp.sum(exp_scores, axis=-1, keepdims=True)
    log_sum = top_score + jnp.log(exp_total)
    soft_probs = (exp_scores / exp_total).astype(jnp.bfloat16)
    attended = jnp.einsum("ngst,tne->snge", soft_probs, value_b, preferred_element_type=jnp.float32)
    attended = attended.reshape(seq_len, -1).astype(jnp.bfloat16)
    kept_vals = (normed_rows, query_raw, key_raw, query_b, key_b, value_b, log_sum, attended)
    return (residual + gather_sum(attended, w_attn), kept_vals)


def attention_backward(
    grad_out, residual, gain_vec, gain_query, gain_key, weights, tables, causal, kept_vals
):
    w_qkv, w_attn = weights
    cosines, sines = tables
    normed_rows, query_raw, key_raw, query_b, key_b, value_b, log_sum, attended = kept_vals
    seq_len = normed_rows.shape[0]
    grad_rows = gather_rows(grad_out.astype(jnp.bfloat16))
    grad_attn = grad_product(attended, grad_rows)
    d_attended = dot_last(grad_rows, w_attn).astype(jnp.bfloat16).reshape(query_b.shape)
    soft_probs = jnp.exp(score_block(query_b, key_b, causal) - log_sum)
    d_probs = jnp.einsum("snge,tne->ngst", d_attended, value_b, preferred_element_type=jnp.float32)
    d_value = jnp.einsum(
        "ngst,snge->tne",
        soft_probs.astype(jnp.bfloat16),
        d_attended,
        preferred_element_type=jnp.float32,
    )
    row_dot = jnp.sum(soft_probs * d_probs, axis=-1, keepdims=True)
    d_scores = (soft_probs * (d_probs - row_dot)).astype(jnp.bfloat16)
    score_scale = HEAD_DIM ** (-0.5)
    d_query = (
        jnp.einsum("ngst,tne->snge", d_scores, key_b, preferred_element_type=jnp.float32)
        * score_scale
    )
    d_key = (
        jnp.einsum("ngst,snge->tne", d_scores, query_b, preferred_element_type=jnp.float32)
        * score_scale
    )
    primal_query, pull_query = jax.vjp(
        lambda raw_rows, gain_vals: head_prep(raw_rows, gain_vals, cosines, sines),
        query_raw,
        gain_query,
    )
    d_query_raw, d_gain_query = pull_query(d_query.reshape(seq_len, -1, HEAD_DIM))
    primal_key, pull_key = jax.vjp(
        lambda raw_rows, gain_vals: head_prep(raw_rows, gain_vals, cosines, sines),
        key_raw,
        gain_key,
    )
    d_key_raw, d_gain_key = pull_key(d_key)
    d_qkv = jnp.concatenate(
        [
            d_query_raw.astype(jnp.bfloat16),
            d_key_raw.astype(jnp.bfloat16),
            d_value.reshape(seq_len, -1).astype(jnp.bfloat16),
        ],
        axis=1,
    )
    d_normed = sum_input_grads(((d_qkv, w_qkv),))
    d_resid, d_gain = norm_back(residual, gain_vec, d_normed)
    grads = (grad_product(normed_rows, d_qkv), grad_attn)
    return (grad_out + d_resid, d_gain, d_gain_query, d_gain_key, grads)


def local(
    tokens, cotangent, master, first_moment, second_moment, gain_master, gain_first, gain_second
):
    dp_count = lax.axis_size("dp")
    tensor_count = lax.axis_size("tensor")
    conv_width = MODEL_DIM // tensor_count
    hidden_width = FEED_HIDDEN // tensor_count
    q_width = QUERY_HEADS // tensor_count * HEAD_DIM
    k_width = KEY_VALUE_HEADS // tensor_count * HEAD_DIM
    mat_shapes = [
        mat_shape
        for segment in weight_layout(MODEL_DIM, conv_width, hidden_width, q_width, k_width)
        for mat_shape in segment
    ]
    spans = [math.prod(mat_shape) // dp_count for mat_shape in mat_shapes]
    plan = FlatPlan(spans)
    owners = block_owners()

    all_rows = to_rows(plan, master)
    pieces = []
    offset = 0
    for number, mat_shape in enumerate(mat_shapes):
        if number == 1:
            pieces.append(None)
            continue
        height = spans[number] // 128
        piece = all_rows[offset : offset + height]
        pieces.append(piece.reshape(mat_shape[0] // dp_count, -1))
        offset += height
    qkv_piece = jnp.concatenate(pieces[6:9], axis=1)

    gap_piece = master[0, 0, spans[0] : spans[0] + spans[1]]
    small = gather_small(jnp.concatenate([gap_piece, gain_master]), "dp")
    kernel = small[:, : spans[1]].reshape(mat_shapes[1])
    kernel = kernel.astype(jnp.bfloat16).astype(jnp.float32)
    gain_vector = gather_small(small[:, spans[1] :], "tensor").transpose(1, 0, 2).reshape(-1)

    gain_one = gain_vector[0:MODEL_DIM]
    gain_two = gain_vector[MODEL_DIM : 2 * MODEL_DIM]
    gain_three = gain_vector[2 * MODEL_DIM : 3 * MODEL_DIM]
    gain_four = gain_vector[3 * MODEL_DIM : 4 * MODEL_DIM]
    gain_query = gain_vector[4 * MODEL_DIM : 4 * MODEL_DIM + HEAD_DIM]
    gain_key = gain_vector[4 * MODEL_DIM + HEAD_DIM : 4 * MODEL_DIM + 2 * HEAD_DIM]

    w_in, w_out, gate_1, up_1, down_1, w_qkv, w_attn, gate_2, up_2, down_2 = fetch_all(
        [pieces[0], pieces[2], *pieces[3:6], qkv_piece, pieces[9], *pieces[10:13]]
    )

    rows_dev = tokens.shape[0]
    positions = (owners[:, None] * rows_dev + jnp.arange(rows_dev)[None, :]).reshape(-1)
    causal = positions[:, None] >= positions[None, :]
    tables = rope_tables_at(positions)

    resid_zero = tokens.astype(jnp.float32)
    mix_weights = (w_in, kernel, w_out)
    ffn_one = (gate_1, up_1, down_1)
    attn_weights = (w_qkv, w_attn)
    ffn_two = (gate_2, up_2, down_2)
    resid_one, kept_mix = mixer_forward(resid_zero, gain_one, mix_weights, owners)
    resid_two, kept_ffn_one = ffn_forward(resid_one, gain_two, ffn_one)
    resid_three, kept_attn = attention_forward(
        resid_two, gain_three, gain_query, gain_key, attn_weights, tables, causal
    )
    resid_four, kept_ffn_two = ffn_forward(
        resid_three, gain_four, ffn_two, jnp.bfloat16
    )

    grad_four = cotangent.astype(jnp.float32)
    grad_three, d_gain_four, grads_ffn_two = ffn_backward(
        grad_four, resid_three, gain_four, ffn_two, kept_ffn_two
    )
    grad_two, d_gain_three, d_gain_query, d_gain_key, grads_attn = attention_backward(
        grad_three,
        resid_two,
        gain_three,
        gain_query,
        gain_key,
        attn_weights,
        tables,
        causal,
        kept_attn,
    )
    grad_one, d_gain_two, grads_ffn_one = ffn_backward(
        grad_two, resid_one, gain_two, ffn_one, kept_ffn_one
    )
    grad_zero, d_gain_one, d_kernel, grads_mix = mixer_backward(
        grad_one, resid_zero, gain_one, mix_weights, kept_mix, owners
    )

    gain_partial = jnp.concatenate(
        [d_gain_one, d_gain_two, d_gain_three, d_gain_four, d_gain_query, d_gain_key]
    )
    gain_count = gain_master.shape[0]
    gain_partial = gain_partial.reshape(dp_count, tensor_count, gain_count).transpose(1, 0, 2)
    gain_column = scatter_small(gain_partial, "tensor")
    small_grad = scatter_small(
        jnp.concatenate([d_kernel.reshape(dp_count, -1), gain_column], axis=1), "dp"
    )
    gap_grad = small_grad[: spans[1]]
    gain_grad = small_grad[spans[1] :]

    grad_qkv, grad_attn = grads_attn
    grad_pieces = [
        grads_mix[0],
        grads_mix[1],
        *grads_ffn_one,
        grad_qkv[:, :q_width],
        grad_qkv[:, q_width : q_width + k_width],
        grad_qkv[:, q_width + k_width :],
        grad_attn,
        *grads_ffn_two,
    ]
    grad_rows = jnp.concatenate([piece.reshape(-1, 128) for piece in grad_pieces], axis=0)
    gap_rows = jnp.concatenate([jnp.zeros(1024 - spans[1], jnp.float32), gap_grad]).reshape(8, 128)
    grad_flat, first_new, second_new, squares = moments_pass(
        plan, master, first_moment, second_moment, grad_rows, gap_rows
    )
    square_sums = jnp.sum(squares, axis=(1, 2))
    mat_count = len(spans)
    weight_sq = square_sums[:mat_count]
    update_sq = square_sums[mat_count + 1 : 2 * mat_count + 1]

    gain_first_new, gain_second_new, gain_update = adam_terms(
        gain_master, gain_grad, gain_first, gain_second
    )
    positions = lax.axis_index(("dp", "tensor")) * gain_count + jnp.arange(
        gain_count, dtype=jnp.int32
    )
    gain_edges = jnp.asarray(
        np.cumsum([0, MODEL_DIM, MODEL_DIM, MODEL_DIM, MODEL_DIM, HEAD_DIM, HEAD_DIM]), jnp.int32
    )
    member = (
        (positions[:, None] >= gain_edges[None, :-1]) & (positions[:, None] < gain_edges[None, 1:])
    ).astype(jnp.float32)
    gain_wsq = jnp.sum((gain_master * gain_master)[:, None] * member, axis=0)
    gain_usq = jnp.sum((gain_update * gain_update)[:, None] * member, axis=0)
    totals = sum_small(jnp.concatenate([weight_sq, gain_wsq, update_sq, gain_usq]))
    norms = jnp.sqrt(totals.reshape(2, -1))
    trust_ratio = norms[0] / (norms[1] + TRUST_EPS)
    ratios = jnp.concatenate([trust_ratio[:mat_count], jnp.zeros(1, jnp.float32)])
    gain_ratio = jnp.sum(member * trust_ratio[None, mat_count:], axis=1)
    new_master, new_copy = weights_pass(plan, master, first_new, second_new, ratios)
    new_gain_master = gain_master - LEARN_RATE * gain_ratio * gain_update
    return (
        resid_four.astype(jnp.bfloat16),
        grad_zero,
        grad_flat,
        new_master,
        first_new,
        second_new,
        new_copy,
        gain_grad,
        new_gain_master,
        gain_first_new,
        gain_second_new,
        norms,
    )


def solution(mesh):
    in_specs = (
        P(("dp", "tensor"), None),
        P(("dp", "tensor"), None),
        P("tensor", "dp", None),
        P("tensor", "dp", None),
        P("tensor", "dp", None),
        P(("dp", "tensor")),
        P(("dp", "tensor")),
        P(("dp", "tensor")),
    )
    out_specs = (
        P(("dp", "tensor"), None),
        P(("dp", "tensor"), None),
        P("tensor", "dp", None),
        P("tensor", "dp", None),
        P("tensor", "dp", None),
        P("tensor", "dp", None),
        P("tensor", "dp", None),
        P(("dp", "tensor")),
        P(("dp", "tensor")),
        P(("dp", "tensor")),
        P(("dp", "tensor")),
        P(),
    )
    return jax.shard_map(local, mesh=mesh, in_specs=in_specs, out_specs=out_specs, check_vma=False)
```

```python
import math

import jax
import jax.numpy as jnp
import numpy as np
from jax import lax
from jax.experimental import pallas as pl
from jax.experimental.pallas import tpu as pltpu
from jax.sharding import PartitionSpec as P

MODEL_DIM = 1536
FEED_HIDDEN = 6912
QUERY_HEADS = 24
KEY_VALUE_HEADS = 8
HEAD_DIM = 64


NORM_EPS = 1e-05
ROPE_BASE = 1000000.0
BETA_FIRST = 0.9
BETA_SECOND = 0.99
ADAM_EPS = 1e-06
DECAY = 0.01
LEARN_RATE = 0.25
TRUST_EPS = 1e-06
MASK_FILL = -1e30


def weight_layout(model_width, conv_width, hidden_width, query_width, key_value_width):
    feed_shapes = [
        (model_width, hidden_width),
        (model_width, hidden_width),
        (hidden_width, model_width),
    ]
    return [
        [(model_width, 3, conv_width), (3, conv_width), (conv_width, model_width)],
        feed_shapes,
        [
            (model_width, query_width),
            (model_width, key_value_width),
            (model_width, key_value_width),
            (query_width, model_width),
        ],
        feed_shapes,
    ]


def rms_norm(values, gain_vec):
    return (
        values * lax.rsqrt(jnp.mean(values * values, axis=-1, keepdims=True) + NORM_EPS) * gain_vec
    )


def rotate(values, cosines, sines):
    half_dim = values.shape[-1] // 2
    first_half = values[..., :half_dim]
    second_half = values[..., half_dim:]
    return jnp.concatenate(
        [first_half * cosines - second_half * sines, second_half * cosines + first_half * sines],
        axis=-1,
    )


def head_prep(raw_rows, gain_vec, cosines, sines):
    sequence_length = raw_rows.shape[0]
    return rotate(
        rms_norm(raw_rows.reshape(sequence_length, -1, HEAD_DIM), gain_vec), cosines, sines
    )


def gated_unit(gate_vals, up_vals):
    return jax.nn.silu(gate_vals) * up_vals


def adam_terms(weight, grad_vals, first_old, second_old):
    first_new = BETA_FIRST * first_old + (1.0 - BETA_FIRST) * grad_vals
    second_new = BETA_SECOND * second_old + (1.0 - BETA_SECOND) * grad_vals * grad_vals
    update = first_new / (jnp.sqrt(second_new) + ADAM_EPS) + DECAY * weight
    return (first_new, second_new, update)


def dot_rows(lhs_rows, rhs_matrix):
    return jnp.dot(lhs_rows, rhs_matrix, preferred_element_type=jnp.float32)


def dot_first(lhs_rows, rhs_rows):
    return lax.dot_general(
        lhs_rows, rhs_rows, (((0,), (0,)), ((), ())), preferred_element_type=jnp.float32
    )


def dot_last(lhs_rows, rhs_matrix):
    return lax.dot_general(
        lhs_rows, rhs_matrix, (((1,), (1,)), ((), ())), preferred_element_type=jnp.float32
    )


def norm_back(values, gain_vec, grad_out):
    primal_out, pullback = jax.vjp(rms_norm, values, gain_vec)
    return pullback(grad_out)


TENSOR_ORDER = (0, 2, 1, 3)


def swap(values, axis_name, bit):
    count = lax.axis_size(axis_name)
    return lax.ppermute(values, axis_name, [(i, i ^ bit) for i in range(count)])


def gather_rows(values):
    if lax.axis_size("tensor") != 4:
        return lax.all_gather(values, "tensor", axis=0, tiled=True)
    far = swap(values, "tensor", 2)
    near = swap(values, "tensor", 1)
    return jnp.concatenate([values, far, near, swap(far, "tensor", 1)], axis=0)


def scatter_rows(partial):
    if lax.axis_size("tensor") != 4:
        return lax.psum_scatter(
            partial.astype(jnp.float32), "tensor", scatter_dimension=0, tiled=True
        )
    own, far, near, cross = jnp.split(partial, 4, axis=0)
    far_sum = far.astype(jnp.float32) + swap(cross, "tensor", 1).astype(jnp.float32)
    far_in = swap(far_sum.astype(partial.dtype), "tensor", 2)
    own_sum = own.astype(jnp.float32) + swap(near, "tensor", 1).astype(jnp.float32)
    return own_sum + far_in.astype(jnp.float32)


def block_owners():
    count = lax.axis_size("tensor")
    own = lax.axis_index("tensor")
    return jnp.stack([own ^ bit for bit in TENSOR_ORDER]) if count == 4 else jnp.arange(count)


def gather_sum(lhs_rows, rhs_matrix):
    return scatter_rows(dot_rows(lhs_rows, rhs_matrix))


def sum_input_grads(grad_pairs, scatter):
    running = None
    for grad_block, weight in grad_pairs:
        product_part = dot_last(grad_block, weight)
        running = product_part if running is None else running + product_part
    return scatter(running.astype(jnp.bfloat16))


def flip_slots(slots, own):
    count = slots.shape[0]
    rest = slots.shape[1:]
    bit = 1
    while bit < count:
        view = slots.reshape((count // (2 * bit), 2, bit) + rest)
        slots = jnp.where((own & bit) != 0, view[:, ::-1], view).reshape((count,) + rest)
        bit *= 2
    return slots


def gather_small(values, axis_name):
    count = lax.axis_size(axis_name)
    slots = [values] + [swap(values, axis_name, bit) for bit in range(1, count)]
    return flip_slots(jnp.stack(slots), lax.axis_index(axis_name))


def scatter_small(values, axis_name):
    count = lax.axis_size(axis_name)
    slots = flip_slots(values, lax.axis_index(axis_name))
    total = slots[0]
    for bit in range(1, count):
        total = total + swap(slots[bit], axis_name, bit)
    return total


def sum_small(values):
    for axis_name in ("tensor", "dp"):
        values = jnp.sum(gather_small(values, axis_name), axis=0)
    return values


def is_grid():
    return lax.axis_size("dp") == 8 and lax.axis_size("tensor") == 4


def dp_bit(bit):
    return (lax.axis_index("dp") // bit) % 2


def pair_up(own, other, bit, axis=0):
    shape = [1] * (own.ndim + 1)
    shape[axis] = 2
    place = lax.broadcasted_iota(jnp.int32, tuple(shape), axis)
    return jnp.where(
        place == dp_bit(bit), jnp.expand_dims(own, axis), jnp.expand_dims(other, axis)
    )


def pick(values, bit, axis, same):
    side = dp_bit(bit) if same else 1 - dp_bit(bit)
    return lax.dynamic_index_in_dim(values, side, axis, keepdims=False)


class Links:
    def __init__(self, depth=2):
        self.depth = depth
        self.past = {1: [], 2: []}

    def send(self, values, bit):
        past = self.past[1 if bit == 1 else 2]
        if len(past) >= self.depth:
            values, _ = lax.optimization_barrier((values, past[-self.depth]))
        got = swap(values, "dp", bit)
        past.append(got)
        return got


class Fetch:
    def __init__(self, links, piece, kind):
        self.links, self.kind = links, kind
        self.rows, self.cols = piece.shape
        self.piece = piece

    def near(self):
        piece = self.piece
        if self.kind == "half":
            view = piece.reshape(self.rows, 2, 2, self.cols // 4)
            own = pick(view, 2, 2, True).reshape(self.rows, -1)
            away = pick(view, 2, 2, False).reshape(self.rows, -1)
        else:
            own = away = piece
        self.held = pair_up(own, self.links.send(away, 2), 2)

    def far(self):
        held = self.piece if self.kind == "rows" else self.held
        self.held = pair_up(held, self.links.send(held, 4), 4)

    def side(self):
        held = self.held
        whole = pair_up(held, self.links.send(held, 1), 1, axis=held.ndim - 2)
        self.whole = whole.reshape(-1, whole.shape[-1])


class Reduce:
    def __init__(self, links, grad, kind):
        self.links, self.kind = links, kind
        lead = (2, 2) if kind == "rows" else (2, 2, 2)
        rows = grad.shape[0] // math.prod(lead)
        self.held = grad.astype(jnp.bfloat16).reshape(lead + (rows, grad.shape[1]))

    def step(self, bit, axis):
        got = self.links.send(pick(self.held, bit, axis, False), bit)
        kept = pick(self.held, bit, axis, True)
        return kept.astype(jnp.float32) + got.astype(jnp.float32)

    def side(self):
        self.held = self.step(1, self.held.ndim - 3).astype(jnp.bfloat16)

    def far(self):
        total = self.step(4, 0)
        self.held = total if self.kind == "rows" else total.astype(jnp.bfloat16)

    def near(self):
        held = self.held
        if self.kind == "whole":
            self.held = self.step(2, 0)
        elif self.kind == "half":
            got = self.links.send(pick(held, 2, 0, False), 2)
            kept = pick(held, 2, 0, True)
            rows, cols = kept.shape
            both = pair_up(
                kept.reshape(rows, 2, cols // 2), got.reshape(rows, 2, cols // 2), 2, axis=2
            )
            self.held = both.reshape(rows, -1).astype(jnp.float32)


def gather_group(values):
    if not is_grid():
        return gather_rows(values)
    half = values.shape[0] // 2
    x_rows = swap(values, "tensor", 2)
    z_rows = swap(values, "dp", 2)
    cross_top = swap(z_rows[:half], "tensor", 2)
    cross_low = swap(x_rows[half:], "dp", 2)
    first = jnp.concatenate([values, x_rows, z_rows], axis=0)
    cross = jnp.concatenate([cross_top, cross_low], axis=0)
    return jnp.concatenate(
        [first, swap(first, "tensor", 1), cross, swap(cross, "tensor", 1)], axis=0
    )


def scatter_group(partial):
    if not is_grid():
        return scatter_rows(partial)
    kind = partial.dtype
    rows = partial.shape[0] // 8
    half = rows // 2
    wide = partial.astype(jnp.float32)
    cross_in = swap(partial[7 * rows :], "tensor", 1)
    first_in = swap(partial[3 * rows : 6 * rows], "tensor", 1)
    cross = wide[6 * rows : 7 * rows] + cross_in.astype(jnp.float32)
    top_in = swap(cross[:half].astype(kind), "tensor", 2)
    low_in = swap(cross[half:].astype(kind), "dp", 2)
    first = wide[: 3 * rows] + first_in.astype(jnp.float32)
    x_sum = jnp.concatenate(
        [first[rows : rows + half], first[rows + half : 2 * rows] + low_in.astype(jnp.float32)],
        axis=0,
    )
    z_sum = jnp.concatenate(
        [first[2 * rows : 2 * rows + half] + top_in.astype(jnp.float32), first[2 * rows + half :]],
        axis=0,
    )
    x_in = swap(x_sum.astype(kind), "tensor", 2)
    z_in = swap(z_sum.astype(kind), "dp", 2)
    return first[:rows] + x_in.astype(jnp.float32) + z_in.astype(jnp.float32)


def fetch_all(pieces, kinds):
    if not is_grid():
        return [lax.all_gather(piece, "dp", axis=0, tiled=True) for piece in pieces]
    links = Links()
    items = [Fetch(links, piece, kind) for piece, kind in zip(pieces, kinds)]
    w_in, w_out, gate_1, up_1, down_1, w_qkv, w_attn, gate_2, up_2, down_2 = items
    w_in.near()
    w_in.far()
    gate_1.near()
    up_1.near()
    w_in.side()
    w_out.near()
    w_out.far()
    gate_1.far()
    w_out.side()
    gate_1.side()
    for before, after in (
        (gate_1, up_1), (up_1, down_1), (down_1, w_qkv), (w_qkv, w_attn),
        (w_attn, gate_2), (gate_2, up_2), (up_2, down_2),
    ):
        if after in (w_qkv, w_attn, gate_2):
            after.near()
        if after is gate_2:
            up_2.near()
        after.far()
        after.side()
    return [item.whole for item in items]


def reduce_matrix(grad, kind, links):
    if not is_grid():
        return lax.psum_scatter(grad.astype(jnp.float32), "dp", scatter_dimension=0, tiled=True)
    item = Reduce(links, grad, kind)
    item.side()
    item.far()
    item.near()
    return item.held


class FlatPlan:
    def __init__(self, spans):
        self.total = sum(spans)
        self.gap = spans[1]
        self.gap_rows, self.gap_lanes = divmod(self.gap, 128)
        self.front = spans[0] // 128
        self.rows = self.front // 3
        self.rest = sum(spans[2:]) // 128
        self.front_blocks = 3
        self.blocks = 3 + -(-(self.rest + self.gap_rows + 1) // self.rows)
        sizes = [spans[0] // 128] + [span // 128 for span in spans[2:]]
        unit = math.gcd(*sizes)
        unit = math.gcd(unit, self.rows)
        while unit % 16 == 0 and unit > 128:
            unit //= 2
        self.unit = unit
        count = len(spans)
        per_block = self.rows // unit
        main = np.full(self.blocks * per_block, count, np.int32)
        edge = np.full(self.blocks * per_block, count, np.int32)
        front_units = self.front // unit
        main[:front_units] = 0
        at = front_units
        edge[at] = 1
        for number in range(2, count):
            units = spans[number] // 128 // unit
            main[at : at + units] = number
            edge[at + 1 : at + units + 1] = number
            at += units
        self.table = np.stack([main, edge])
        self.per_block = per_block
        self.count = count


def flat_spec(plan):
    return pl.BlockSpec((1, 1, plan.rows * 128), lambda i, *_: (0, 0, i))


def rows_spec(plan):
    return pl.BlockSpec((plan.rows, 128), lambda i, *_: (i, 0))


def lane_ids(rows):
    return lax.broadcasted_iota(jnp.int32, (rows, 128), 1)


def to_rows(plan, flat):
    rows, lanes, skip = plan.rows, plan.gap_lanes, plan.gap_rows
    last = -(-plan.total // 1024) - 1

    def body(cur_ref, next_ref, out_ref, work_ref):
        cur = cur_ref[0, 0].reshape(rows, 128)
        work_ref[0:rows, :] = pltpu.roll(cur, 128 - lanes, 1)
        work_ref[rows : rows + 8, :] = pltpu.roll(next_ref[0, 0].reshape(8, 128), 128 - lanes, 1)
        low = work_ref[skip : skip + rows, :]
        high = work_ref[skip + 1 : skip + 1 + rows, :]
        moved = jnp.where(lane_ids(rows) < 128 - lanes, low, high)
        front = pl.program_id(0) < plan.front_blocks
        out_ref[...] = jnp.where(front, cur, moved).astype(jnp.bfloat16)

    return pl.pallas_call(
        body,
        name="to_rows",
        grid=(plan.blocks,),
        out_shape=jax.ShapeDtypeStruct((plan.blocks * rows, 128), jnp.bfloat16),
        in_specs=[
            flat_spec(plan),
            pl.BlockSpec(
                (1, 1, 1024), lambda i: (0, 0, jnp.minimum((i + 1) * (rows // 8), last))
            ),
        ],
        out_specs=rows_spec(plan),
        scratch_shapes=[pltpu.VMEM((rows + 8, 128), jnp.float32)],
        cost_estimate=pl.CostEstimate(
            flops=plan.total, bytes_accessed=6 * plan.total, transcendentals=0
        ),
    )(flat, flat)


def edge_mask(plan):
    place = lax.broadcasted_iota(jnp.int32, (8, 128), 0) * 128 + lane_ids(8)
    return (place < plan.gap) & (pl.program_id(0) >= plan.front_blocks)


def moments_pass(plan, weight, first_old, second_old, grad_rows, gap_rows):
    rows, lanes, skip, unit = plan.rows, plan.gap_lanes, plan.gap_rows, plan.unit

    def body(
        table, w_ref, m_ref, v_ref, g_ref, prev_ref, gap_ref,
        grad_ref, first_ref, second_ref, sums_ref, work_ref,
    ):
        step = pl.program_id(0)

        @pl.when(step == 0)
        def _():
            sums_ref[...] = jnp.zeros_like(sums_ref)

        cur = g_ref[...]
        prev = jnp.where(step == plan.front_blocks, gap_ref[...], prev_ref[...])
        work_ref[0:8, :] = pltpu.roll(prev, lanes, 1)
        work_ref[8 : 8 + rows, :] = pltpu.roll(cur, lanes, 1)
        low = work_ref[7 - skip : 7 - skip + rows, :]
        high = work_ref[8 - skip : 8 - skip + rows, :]
        moved = jnp.where(lane_ids(rows) < lanes, low, high)
        grad = jnp.where(step < plan.front_blocks, cur, moved)
        w = w_ref[0, 0].reshape(rows, 128)
        first_new, second_new, update = adam_terms(
            w, grad, m_ref[0, 0].reshape(rows, 128), v_ref[0, 0].reshape(rows, 128)
        )
        grad_ref[0, 0] = grad.reshape(rows * 128)
        first_ref[0, 0] = first_new.reshape(rows * 128)
        second_ref[0, 0] = second_new.reshape(rows * 128)
        mask = edge_mask(plan)
        for part in range(plan.per_block):
            main = table[0, step * plan.per_block + part]
            edge = table[1, step * plan.per_block + part]
            for base, values in ((0, w), (plan.count + 1, update)):
                square = values[part * unit : (part + 1) * unit]
                square = square * square
                inner = jnp.where(mask, 0.0, square[0:8])
                for at in range(8, unit, 8):
                    inner = inner + square[at : at + 8]
                sums_ref[base + main] += inner
                sums_ref[base + edge] += jnp.where(mask, square[0:8], 0.0)

    lin = flat_spec(plan)
    flat = jax.ShapeDtypeStruct((1, 1, plan.total), jnp.float32)
    sums = 2 * (plan.count + 1)
    return pl.pallas_call(
        body,
        name="moments_pass",
        grid_spec=pltpu.PrefetchScalarGridSpec(
            num_scalar_prefetch=1,
            grid=(plan.blocks,),
            in_specs=[
                lin, lin, lin, rows_spec(plan),
                pl.BlockSpec(
                    (8, 128), lambda i, *_: (jnp.maximum(i * (rows // 8) - 1, 0), 0)
                ),
                pl.BlockSpec((8, 128), lambda i, *_: (0, 0)),
            ],
            out_specs=[lin, lin, lin, pl.BlockSpec((sums, 8, 128), lambda i, *_: (0, 0, 0))],
            scratch_shapes=[pltpu.VMEM((rows + 8, 128), jnp.float32)],
        ),
        out_shape=[flat, flat, flat, jax.ShapeDtypeStruct((sums, 8, 128), jnp.float32)],
        cost_estimate=pl.CostEstimate(
            flops=20 * plan.total, bytes_accessed=28 * plan.total, transcendentals=plan.total
        ),
    )(jnp.asarray(plan.table), weight, first_old, second_old, grad_rows, grad_rows, gap_rows)


def weights_pass(plan, weight, first_new, second_new, ratios):
    rows, unit = plan.rows, plan.unit

    def body(table, w_ref, m_ref, v_ref, ratio_ref, new_ref, copy_ref):
        step = pl.program_id(0)
        mask = edge_mask(plan)
        pieces = []
        w = w_ref[0, 0].reshape(rows, 128)
        first, second = m_ref[0, 0].reshape(rows, 128), v_ref[0, 0].reshape(rows, 128)
        update = first / (jnp.sqrt(second) + ADAM_EPS) + DECAY * w
        for part in range(plan.per_block):
            main = ratio_ref[table[0, step * plan.per_block + part]]
            edge = ratio_ref[table[1, step * plan.per_block + part]]
            here = slice(part * unit, part * unit + 8)
            pieces.append(w[here] - LEARN_RATE * jnp.where(mask, edge, main) * update[here])
            here = slice(part * unit + 8, (part + 1) * unit)
            pieces.append(w[here] - LEARN_RATE * main * update[here])
        fresh = jnp.concatenate(pieces, axis=0)
        new_ref[0, 0] = fresh.reshape(rows * 128)
        copy_ref[0, 0] = fresh.reshape(rows * 128).astype(jnp.bfloat16)

    lin = flat_spec(plan)
    shape = (1, 1, plan.total)
    return pl.pallas_call(
        body,
        name="weights_pass",
        grid_spec=pltpu.PrefetchScalarGridSpec(
            num_scalar_prefetch=1,
            grid=(plan.blocks,),
            in_specs=[lin, lin, lin, pl.BlockSpec(memory_space=pltpu.SMEM)],
            out_specs=[lin, lin],
        ),
        out_shape=[
            jax.ShapeDtypeStruct(shape, jnp.float32),
            jax.ShapeDtypeStruct(shape, jnp.bfloat16),
        ],
        cost_estimate=pl.CostEstimate(
            flops=8 * plan.total, bytes_accessed=18 * plan.total, transcendentals=plan.total
        ),
    )(jnp.asarray(plan.table), weight, first_new, second_new, ratios)


def neighbour_rows(edge_rows, owners, offset):
    result = []
    for here in range(edge_rows.shape[0]):
        picked = jnp.zeros_like(edge_rows[0])
        for there in range(edge_rows.shape[0]):
            hit = owners[there] == owners[here] + offset
            picked = jnp.where(hit, edge_rows[there], picked)
        result.append(picked)
    return jnp.stack(result)


def mixer_forward(residual, gain_vec, weights, owners):
    w_in, kernel, w_out = weights
    conv_width = kernel.shape[1]
    normed_rows = gather_rows(rms_norm(residual, gain_vec).astype(jnp.bfloat16))
    projected = dot_rows(normed_rows, w_in).reshape(owners.shape[0], -1, 3 * conv_width)
    gate_b = projected[:, :, :conv_width]
    gate_c = projected[:, :, conv_width : 2 * conv_width]
    values = projected[:, :, 2 * conv_width :]
    product = gate_b * values
    padded = jnp.concatenate([neighbour_rows(product[:, -2:], owners, -1), product], axis=1)
    conv_mixed = (
        kernel[0] * padded[:, :-2] + kernel[1] * padded[:, 1:-1] + kernel[2] * padded[:, 2:]
    )
    conv_out = (gate_c * conv_mixed).astype(jnp.bfloat16).reshape(-1, conv_width)
    kept_vals = (normed_rows, gate_b, gate_c, values, padded, conv_mixed, conv_out)
    return (residual + gather_sum(conv_out, w_out), kept_vals)


def mixer_backward(grad_out, residual, gain_vec, weights, kept_vals, owners, links):
    w_in, kernel, w_out = weights
    normed_rows, gate_b, gate_c, values, padded, conv_mixed, conv_out = kept_vals
    grad_rows = gather_rows(grad_out.astype(jnp.bfloat16))
    grad_out_w = grad_product(conv_out, grad_rows, "whole", links)
    d_conv = dot_last(grad_rows, w_out).reshape(conv_mixed.shape)
    d_gate_c = d_conv * conv_mixed
    d_mixed = d_conv * gate_c
    padded_grad = jnp.concatenate([d_mixed, neighbour_rows(d_mixed[:, :2], owners, 1)], axis=1)
    d_product = (
        kernel[0] * padded_grad[:, 2:]
        + kernel[1] * padded_grad[:, 1:-1]
        + kernel[2] * padded_grad[:, :-2]
    )
    d_kernel = jnp.stack(
        [
            jnp.sum(d_mixed * padded[:, :-2], axis=(0, 1)),
            jnp.sum(d_mixed * padded[:, 1:-1], axis=(0, 1)),
            jnp.sum(d_mixed * padded[:, 2:], axis=(0, 1)),
        ]
    )
    d_proj = jnp.concatenate(
        [
            (d_product * values).astype(jnp.bfloat16),
            d_gate_c.astype(jnp.bfloat16),
            (d_product * gate_b).astype(jnp.bfloat16),
        ],
        axis=-1,
    ).reshape(normed_rows.shape[0], -1)
    d_normed = sum_input_grads(((d_proj, w_in),), scatter_rows)
    d_resid, d_gain = norm_back(residual, gain_vec, d_normed)
    grads = (grad_product(normed_rows, d_proj, "whole", links), grad_out_w)
    return (grad_out + d_resid, d_gain, d_kernel, grads)


def grad_product(lhs_rows, rhs_rows, kind, links):
    return reduce_matrix(dot_first(lhs_rows, rhs_rows).astype(jnp.bfloat16), kind, links)


def ffn_forward(residual, gain_vec, weights, send_type=jnp.float32):
    w_gate, w_up, w_down = weights
    normed_rows = gather_group(rms_norm(residual, gain_vec).astype(jnp.bfloat16))
    gate_vals = dot_rows(normed_rows, w_gate)
    up_vals = dot_rows(normed_rows, w_up)
    hidden = gated_unit(gate_vals, up_vals).astype(jnp.bfloat16)
    branch = scatter_group(dot_rows(hidden, w_down).astype(send_type))
    return (residual + branch, (normed_rows, gate_vals, up_vals, hidden))


def ffn_backward(grad_out, residual, gain_vec, weights, kept_vals, links):
    w_gate, w_up, w_down = weights
    normed_rows, gate_vals, up_vals, hidden = kept_vals
    grad_rows = gather_group(grad_out.astype(jnp.bfloat16))
    grad_down = grad_product(hidden, grad_rows, "rows", links)
    d_hidden = dot_last(grad_rows, w_down)
    primal_out, pullback = jax.vjp(gated_unit, gate_vals, up_vals)
    d_gate, d_up = pullback(d_hidden)
    d_gate = d_gate.astype(jnp.bfloat16)
    d_up = d_up.astype(jnp.bfloat16)
    d_normed = sum_input_grads(((d_gate, w_gate), (d_up, w_up)), scatter_group)
    d_resid, d_gain = norm_back(residual, gain_vec, d_normed)
    grad_gate = grad_product(normed_rows, d_gate, "half", links)
    grads = (grad_gate, grad_product(normed_rows, d_up, "half", links), grad_down)
    return (grad_out + d_resid, d_gain, grads)


def rope_tables_at(positions):
    inv_freq = ROPE_BASE ** (-jnp.arange(0, HEAD_DIM, 2, dtype=jnp.float32) / HEAD_DIM)
    angles = positions.astype(jnp.float32)[:, None] * inv_freq[None, :]
    return (jnp.cos(angles)[:, None, :], jnp.sin(angles)[:, None, :])


def score_block(query_b, key_b, causal):
    scores = jnp.einsum(
        "snge,tne->ngst", query_b, key_b, preferred_element_type=jnp.float32
    ) * HEAD_DIM ** (-0.5)
    return jnp.where(causal, scores, MASK_FILL)


def attention_forward(residual, gain_vec, gain_query, gain_key, weights, tables, causal):
    w_qkv, w_attn = weights
    cosines, sines = tables
    normed_rows = gather_rows(rms_norm(residual, gain_vec).astype(jnp.bfloat16))
    seq_len = normed_rows.shape[0]
    q_width = w_attn.shape[0]
    k_width = (w_qkv.shape[1] - q_width) // 2
    q_heads = q_width // HEAD_DIM
    kv_heads = k_width // HEAD_DIM
    projected = dot_rows(normed_rows, w_qkv)
    query_raw = projected[:, :q_width]
    key_raw = projected[:, q_width : q_width + k_width]
    value_b = (
        projected[:, q_width + k_width :]
        .astype(jnp.bfloat16)
        .reshape(seq_len, kv_heads, HEAD_DIM)
    )
    query_b = (
        head_prep(query_raw, gain_query, cosines, sines)
        .astype(jnp.bfloat16)
        .reshape(seq_len, kv_heads, q_heads // kv_heads, HEAD_DIM)
    )
    key_b = head_prep(key_raw, gain_key, cosines, sines).astype(jnp.bfloat16)
    scores = score_block(query_b, key_b, causal)
    top_score = jnp.max(scores, axis=-1, keepdims=True)
    exp_scores = jnp.exp(scores - top_score)
    exp_total = jnp.sum(exp_scores, axis=-1, keepdims=True)
    log_sum = top_score + jnp.log(exp_total)
    soft_probs = (exp_scores / exp_total).astype(jnp.bfloat16)
    attended = jnp.einsum("ngst,tne->snge", soft_probs, value_b, preferred_element_type=jnp.float32)
    attended = attended.reshape(seq_len, -1).astype(jnp.bfloat16)
    kept_vals = (normed_rows, query_raw, key_raw, query_b, key_b, value_b, log_sum, attended)
    return (residual + gather_sum(attended, w_attn), kept_vals)


def attention_backward(
    grad_out, residual, gain_vec, gain_query, gain_key, weights, tables, causal, kept_vals, links
):
    w_qkv, w_attn = weights
    cosines, sines = tables
    normed_rows, query_raw, key_raw, query_b, key_b, value_b, log_sum, attended = kept_vals
    seq_len = normed_rows.shape[0]
    grad_rows = gather_rows(grad_out.astype(jnp.bfloat16))
    grad_attn = grad_product(attended, grad_rows, "whole", links)
    d_attended = dot_last(grad_rows, w_attn).astype(jnp.bfloat16).reshape(query_b.shape)
    soft_probs = jnp.exp(score_block(query_b, key_b, causal) - log_sum)
    d_probs = jnp.einsum("snge,tne->ngst", d_attended, value_b, preferred_element_type=jnp.float32)
    d_value = jnp.einsum(
        "ngst,snge->tne",
        soft_probs.astype(jnp.bfloat16),
        d_attended,
        preferred_element_type=jnp.float32,
    )
    row_dot = jnp.sum(soft_probs * d_probs, axis=-1, keepdims=True)
    d_scores = (soft_probs * (d_probs - row_dot)).astype(jnp.bfloat16)
    score_scale = HEAD_DIM ** (-0.5)
    d_query = (
        jnp.einsum("ngst,tne->snge", d_scores, key_b, preferred_element_type=jnp.float32)
        * score_scale
    )
    d_key = (
        jnp.einsum("ngst,snge->tne", d_scores, query_b, preferred_element_type=jnp.float32)
        * score_scale
    )
    primal_query, pull_query = jax.vjp(
        lambda raw_rows, gain_vals: head_prep(raw_rows, gain_vals, cosines, sines),
        query_raw,
        gain_query,
    )
    d_query_raw, d_gain_query = pull_query(d_query.reshape(seq_len, -1, HEAD_DIM))
    primal_key, pull_key = jax.vjp(
        lambda raw_rows, gain_vals: head_prep(raw_rows, gain_vals, cosines, sines),
        key_raw,
        gain_key,
    )
    d_key_raw, d_gain_key = pull_key(d_key)
    d_qkv = jnp.concatenate(
        [
            d_query_raw.astype(jnp.bfloat16),
            d_key_raw.astype(jnp.bfloat16),
            d_value.reshape(seq_len, -1).astype(jnp.bfloat16),
        ],
        axis=1,
    )
    d_normed = sum_input_grads(((d_qkv, w_qkv),), scatter_rows)
    d_resid, d_gain = norm_back(residual, gain_vec, d_normed)
    grads = (grad_product(normed_rows, d_qkv, "whole", links), grad_attn)
    return (grad_out + d_resid, d_gain, d_gain_query, d_gain_key, grads)


def local(
    tokens, cotangent, master, first_moment, second_moment, gain_master, gain_first, gain_second
):
    dp_count = lax.axis_size("dp")
    tensor_count = lax.axis_size("tensor")
    conv_width = MODEL_DIM // tensor_count
    hidden_width = FEED_HIDDEN // tensor_count
    q_width = QUERY_HEADS // tensor_count * HEAD_DIM
    k_width = KEY_VALUE_HEADS // tensor_count * HEAD_DIM
    mat_shapes = [
        mat_shape
        for segment in weight_layout(MODEL_DIM, conv_width, hidden_width, q_width, k_width)
        for mat_shape in segment
    ]
    spans = [math.prod(mat_shape) // dp_count for mat_shape in mat_shapes]
    plan = FlatPlan(spans)
    owners = block_owners()

    all_rows = to_rows(plan, master)
    pieces = []
    offset = 0
    for number, mat_shape in enumerate(mat_shapes):
        if number == 1:
            pieces.append(None)
            continue
        height = spans[number] // 128
        piece = all_rows[offset : offset + height]
        pieces.append(piece.reshape(mat_shape[0] // dp_count, -1))
        offset += height
    qkv_piece = jnp.concatenate(pieces[6:9], axis=1)

    gap_piece = master[0, 0, spans[0] : spans[0] + spans[1]]
    small = gather_small(jnp.concatenate([gap_piece, gain_master]), "dp")
    kernel = small[:, : spans[1]].reshape(mat_shapes[1])
    kernel = kernel.astype(jnp.bfloat16).astype(jnp.float32)
    gain_vector = gather_small(small[:, spans[1] :], "tensor").transpose(1, 0, 2).reshape(-1)

    gain_one = gain_vector[0:MODEL_DIM]
    gain_two = gain_vector[MODEL_DIM : 2 * MODEL_DIM]
    gain_three = gain_vector[2 * MODEL_DIM : 3 * MODEL_DIM]
    gain_four = gain_vector[3 * MODEL_DIM : 4 * MODEL_DIM]
    gain_query = gain_vector[4 * MODEL_DIM : 4 * MODEL_DIM + HEAD_DIM]
    gain_key = gain_vector[4 * MODEL_DIM + HEAD_DIM : 4 * MODEL_DIM + 2 * HEAD_DIM]

    w_in, w_out, gate_1, up_1, down_1, w_qkv, w_attn, gate_2, up_2, down_2 = fetch_all(
        [pieces[0], pieces[2], *pieces[3:6], qkv_piece, pieces[9], *pieces[10:13]],
        ["whole", "whole", "half", "half", "rows", "whole", "whole", "half", "half", "rows"],
    )
    links = Links()

    rows_dev = tokens.shape[0]
    positions = (owners[:, None] * rows_dev + jnp.arange(rows_dev)[None, :]).reshape(-1)
    causal = positions[:, None] >= positions[None, :]
    tables = rope_tables_at(positions)

    resid_zero = tokens.astype(jnp.float32)
    mix_weights = (w_in, kernel, w_out)
    ffn_one = (gate_1, up_1, down_1)
    attn_weights = (w_qkv, w_attn)
    ffn_two = (gate_2, up_2, down_2)
    resid_one, kept_mix = mixer_forward(resid_zero, gain_one, mix_weights, owners)
    resid_two, kept_ffn_one = ffn_forward(resid_one, gain_two, ffn_one)
    resid_three, kept_attn = attention_forward(
        resid_two, gain_three, gain_query, gain_key, attn_weights, tables, causal
    )
    resid_four, kept_ffn_two = ffn_forward(
        resid_three, gain_four, ffn_two, jnp.bfloat16
    )

    grad_four = cotangent.astype(jnp.float32)
    grad_three, d_gain_four, grads_ffn_two = ffn_backward(
        grad_four, resid_three, gain_four, ffn_two, kept_ffn_two, links
    )
    grad_two, d_gain_three, d_gain_query, d_gain_key, grads_attn = attention_backward(
        grad_three,
        resid_two,
        gain_three,
        gain_query,
        gain_key,
        attn_weights,
        tables,
        causal,
        kept_attn,
        links,
    )
    grad_one, d_gain_two, grads_ffn_one = ffn_backward(
        grad_two, resid_one, gain_two, ffn_one, kept_ffn_one, links
    )
    grad_zero, d_gain_one, d_kernel, grads_mix = mixer_backward(
        grad_one, resid_zero, gain_one, mix_weights, kept_mix, owners, links
    )

    gain_partial = jnp.concatenate(
        [d_gain_one, d_gain_two, d_gain_three, d_gain_four, d_gain_query, d_gain_key]
    )
    gain_count = gain_master.shape[0]
    gain_partial = gain_partial.reshape(dp_count, tensor_count, gain_count).transpose(1, 0, 2)
    gain_column = scatter_small(gain_partial, "tensor")
    small_grad = scatter_small(
        jnp.concatenate([d_kernel.reshape(dp_count, -1), gain_column], axis=1), "dp"
    )
    gap_grad = small_grad[: spans[1]]
    gain_grad = small_grad[spans[1] :]

    grad_qkv, grad_attn = grads_attn
    grad_pieces = [
        grads_mix[0],
        grads_mix[1],
        *grads_ffn_one,
        grad_qkv[:, :q_width],
        grad_qkv[:, q_width : q_width + k_width],
        grad_qkv[:, q_width + k_width :],
        grad_attn,
        *grads_ffn_two,
    ]
    grad_rows = jnp.concatenate([piece.reshape(-1, 128) for piece in grad_pieces], axis=0)
    gap_rows = jnp.concatenate([jnp.zeros(1024 - spans[1], jnp.float32), gap_grad]).reshape(8, 128)
    grad_flat, first_new, second_new, squares = moments_pass(
        plan, master, first_moment, second_moment, grad_rows, gap_rows
    )
    square_sums = jnp.sum(squares, axis=(1, 2))
    mat_count = len(spans)
    weight_sq = square_sums[:mat_count]
    update_sq = square_sums[mat_count + 1 : 2 * mat_count + 1]

    gain_first_new, gain_second_new, gain_update = adam_terms(
        gain_master, gain_grad, gain_first, gain_second
    )
    positions = lax.axis_index(("dp", "tensor")) * gain_count + jnp.arange(
        gain_count, dtype=jnp.int32
    )
    gain_edges = jnp.asarray(
        np.cumsum([0, MODEL_DIM, MODEL_DIM, MODEL_DIM, MODEL_DIM, HEAD_DIM, HEAD_DIM]), jnp.int32
    )
    member = (
        (positions[:, None] >= gain_edges[None, :-1]) & (positions[:, None] < gain_edges[None, 1:])
    ).astype(jnp.float32)
    gain_wsq = jnp.sum((gain_master * gain_master)[:, None] * member, axis=0)
    gain_usq = jnp.sum((gain_update * gain_update)[:, None] * member, axis=0)
    totals = sum_small(jnp.concatenate([weight_sq, gain_wsq, update_sq, gain_usq]))
    norms = jnp.sqrt(totals.reshape(2, -1))
    trust_ratio = norms[0] / (norms[1] + TRUST_EPS)
    ratios = jnp.concatenate([trust_ratio[:mat_count], jnp.zeros(1, jnp.float32)])
    gain_ratio = jnp.sum(member * trust_ratio[None, mat_count:], axis=1)
    new_master, new_copy = weights_pass(plan, master, first_new, second_new, ratios)
    new_gain_master = gain_master - LEARN_RATE * gain_ratio * gain_update
    return (
        resid_four.astype(jnp.bfloat16),
        grad_zero,
        grad_flat,
        new_master,
        first_new,
        second_new,
        new_copy,
        gain_grad,
        new_gain_master,
        gain_first_new,
        gain_second_new,
        norms,
    )


def solution(mesh):
    in_specs = (
        P(("dp", "tensor"), None),
        P(("dp", "tensor"), None),
        P("tensor", "dp", None),
        P("tensor", "dp", None),
        P("tensor", "dp", None),
        P(("dp", "tensor")),
        P(("dp", "tensor")),
        P(("dp", "tensor")),
    )
    out_specs = (
        P(("dp", "tensor"), None),
        P(("dp", "tensor"), None),
        P("tensor", "dp", None),
        P("tensor", "dp", None),
        P("tensor", "dp", None),
        P("tensor", "dp", None),
        P("tensor", "dp", None),
        P(("dp", "tensor")),
        P(("dp", "tensor")),
        P(("dp", "tensor")),
        P(("dp", "tensor")),
        P(),
    )
    return jax.shard_map(local, mesh=mesh, in_specs=in_specs, out_specs=out_specs, check_vma=False)
```
